1024 devices in a mesh: seq: 64 (over z, core), head: 16 (over y, x).
Axes of the slice: x: 4, y: 4, z: 32, core: 2. Of those that a mesh axis runs over, the one named last changes fastest.
Arguments:
- queries: bfloat16 [16384, 8192], P('seq', 'head'), may hold values from -6 to 6
- key_input: bfloat16 [16384, 8192], P('seq', 'head'), may hold values from -6 to 6
- value_input: bfloat16 [16384, 8192], P('seq', 'head'), may hold values from -6 to 6
- out_gate: bfloat16 [16384, 8192], P('seq', 'head'), may hold values from -8 to 8
- log_decay: float32 [64, 16384], P('head', 'seq'), may hold values from -1 to 0, as said below
- norm_gain: float32 [8192], P('head'), may hold values from 0.1 to 1.9
- features: bfloat16 [16384, 6144], P('seq', 'head'), may hold values from -6 to 6
- expert_ids: int32 [16384, 2], P('seq'), may hold values from 0 to 31, as said below
- route_weight: float32 [16384, 2], P('seq'), may hold values from 0.25 to 1
- placement: int32 [4], replicated, may hold values from 0 to 31, as said below
- gate_weight: bfloat16 [6144, 36864], P('head', 'seq'), may hold values from -0.078125 to 0.078125
- up_weight: bfloat16 [6144, 36864], P('head', 'seq'), may hold values from -0.078125 to 0.078125
- down_weight: bfloat16 [36864, 6144], P('seq', 'head'), may hold values from -0.0625 to 0.0625
Outputs:
- attention_out: bfloat16 [16384, 8192], P('seq', 'head')
- moe_out: bfloat16 [16384, 6144], P('seq', 'head')
The draws below stay inside these ranges and needn't reach their ends.
Inputs may be any that keep to these rules, and one draw needn't show every extreme that they name: `expert_ids`: in each aligned block of 256 tokens, each expert named in placement is named by at most 8 tokens, and the same one of them by exactly 8 tokens in every block; the two ids of a token differ. `placement`: 4 different expert numbers, among them always 0 and 31. `log_decay`: every entry is negative.
All inputs are finite; a program needn't handle non-finite values.
Results may differ from the reference program's by a relative error of at most 0.0058.
Values may be sent and summed in bfloat16 or wider, within the bound.
No kernel may reach another device: no remote copies, remote signals or barrier semaphores. Data moves between devices by JAX's collectives and lax.ppermute only.
A program may use at most 64 MiB of HBM per device.

```python
import jax
import jax.numpy as jnp
from jax import lax

D = 6144
HEADS = 64
HEAD_DIM = 128
FF = 9216
EXPERTS = 32
EXP_FLY = 4
TOK_DEV = 256
CAP = 8
SEQUENCE_TOKENS = 16384
N_SEQ = 64


def draw_log_decay(key, part):
    random_keys = jax.random.split(jax.random.fold_in(key, 11), 6)
    blocks = SEQUENCE_TOKENS // TOK_DEV
    fast_share = 0.5
    fast = jax.random.uniform(random_keys[0], (HEADS, 1), jnp.float32) < fast_share
    fast_rate = jnp.exp(jax.random.uniform(random_keys[1], (HEADS, 1), jnp.float32, jnp.log(1.0 / 50.0), jnp.log(1.0 / 30.0)))
    slow_rate = 0.25 / SEQUENCE_TOKENS * jnp.ones((HEADS, 1), jnp.float32)
    decay_rate = jnp.where(fast, fast_rate, slow_rate)
    block_decay_factor = jax.random.uniform(random_keys[2], (HEADS, blocks, 1), jnp.float32, 1.0, 2.0)
    block_decay_factor = jnp.broadcast_to(block_decay_factor, (HEADS, blocks, TOK_DEV)).reshape(HEADS, SEQUENCE_TOKENS)
    token_decay_factor = jnp.exp(jax.random.uniform(random_keys[3], (HEADS, SEQUENCE_TOKENS), jnp.float32, jnp.log(0.5), jnp.log(2.0)))
    spike_locations = jax.random.randint(random_keys[4], (3,), 0, SEQUENCE_TOKENS)
    spike_depth = jnp.log(jax.random.uniform(random_keys[5], (3,), jnp.float32, 0.5, 0.8))
    token_positions = jnp.arange(SEQUENCE_TOKENS)
    decay_spikes = jnp.sum(jnp.where(token_positions[None, :] == spike_locations[:, None], spike_depth[:, None], 0.0), axis=0)
    return -decay_rate * block_decay_factor * token_decay_factor + decay_spikes[None, :]


def route_plan(key):
    plan_keys = jax.random.split(jax.random.fold_in(key, 5), 2)
    middle = (jax.random.permutation(plan_keys[0], EXPERTS - 2) + 1)[:EXP_FLY - 2].astype(jnp.int32)
    ends = jnp.array([0, EXPERTS - 1], dtype=jnp.int32)
    chosen = jnp.concatenate([ends, middle], axis=0)
    order = jax.random.permutation(plan_keys[1], EXP_FLY)
    return chosen[order].astype(jnp.int32)


def draw_placement(key, part):
    return route_plan(key)


def draw_expert_ids(key, part):
    placement = route_plan(key)
    blocks = SEQUENCE_TOKENS // TOK_DEV
    random_keys = jax.random.split(jax.random.fold_in(key, 9), 4)
    full_slot = jax.random.randint(random_keys[0], (), 0, EXP_FLY)
    loads = jax.random.randint(random_keys[1], (blocks, EXP_FLY), CAP // 4, CAP + 1)
    loads = jnp.where(jnp.arange(EXP_FLY)[None, :] == full_slot, CAP, loads)
    rest = 2 * TOK_DEV - jnp.sum(loads, axis=1)
    others = EXPERTS - EXP_FLY
    base = rest // others
    extra = rest % others
    in_flight = (jnp.arange(EXPERTS)[:, None] == placement[None, :]).astype(jnp.int32)
    flying = jnp.sum(in_flight, axis=1)
    other_rank = jnp.cumsum(1 - flying) - 1
    counts_other = base[:, None] + (other_rank[None, :] < extra[:, None]).astype(jnp.int32)
    counts_fly = jnp.sum(in_flight[None, :, :] * loads[:, None, :], axis=2)
    counts = jnp.where(flying[None, :] == 1, counts_fly, counts_other)
    ends = jnp.cumsum(counts, axis=1)
    position = jnp.arange(2 * TOK_DEV)
    listed = jnp.sum((position[None, :, None] >= ends[:, None, :]).astype(jnp.int32), axis=2)
    pairs = jnp.stack([listed[:, :TOK_DEV], listed[:, TOK_DEV:]], axis=-1)
    orders = jax.vmap(lambda sub: jax.random.permutation(sub, TOK_DEV))(jax.random.split(random_keys[2], blocks))
    pairs = jnp.take_along_axis(pairs, orders[:, :, None], axis=1)
    flip = jax.random.randint(random_keys[3], (blocks, TOK_DEV, 1), 0, 2)
    pairs = jnp.where(flip == 1, pairs[:, :, ::-1], pairs)
    return pairs.reshape(SEQUENCE_TOKENS, 2).astype(jnp.int32)


def steps_of(key, shape, cuts, low, high):
    factor_of, own = 1.0, jax.random.fold_in(key, 6)
    for axis_at, parts in cuts:
        draws = jnp.exp(jax.random.uniform(jax.random.fold_in(own, axis_at), (parts,), jnp.float32, low / len(cuts), high / len(cuts)))
        factor_of = factor_of * jnp.repeat(draws, shape[axis_at] // parts).reshape([-1 if axis == axis_at else 1 for axis in range(len(shape))])
    return factor_of


def scatter_about(own_key, shape, scale, reach, cuts=(), kind=jnp.bfloat16):
    entries = scale * jax.random.normal(own_key, shape, jnp.float32)
    if cuts:
        entries = entries * steps_of(own_key, shape, cuts, -0.22, 0.18)
    return jnp.clip(entries, -reach, reach).astype(kind)


def setup_inputs(seed: int = 0) -> dict:
    seeds = jax.random.split(jax.random.key(seed), 14)
    queries = scatter_about(seeds[0], (SEQUENCE_TOKENS, HEADS * HEAD_DIM), 1.0, 6.0, ((0, 64), (1, 16)))
    key_input = scatter_about(seeds[1], (SEQUENCE_TOKENS, HEADS * HEAD_DIM), 1.0, 6.0, ((0, 64), (1, 16)))
    value_input = scatter_about(seeds[2], (SEQUENCE_TOKENS, HEADS * HEAD_DIM), 1.0, 6.0, ((0, 64), (1, 16)))
    out_gate = scatter_about(seeds[3], (SEQUENCE_TOKENS, HEADS * HEAD_DIM), 2.0, 8.0, ((0, 64), (1, 16)))
    log_decay = draw_log_decay(jax.random.fold_in(seeds[13], 71), 0)
    norm_gain = jnp.clip(1.0 + 0.18 * jax.random.normal(seeds[5], (HEADS * HEAD_DIM,), jnp.float32), 0.1, 1.9)
    features = scatter_about(seeds[6], (SEQUENCE_TOKENS, D), 1.0, 6.0, ((0, 64), (1, 16)))
    expert_ids = draw_expert_ids(jax.random.fold_in(seeds[13], 71), 0)
    route_weight = jnp.clip(0.25 + 0.75 * jax.random.uniform(seeds[8], (SEQUENCE_TOKENS, 2), jnp.float32) ** steps_of(seeds[8], (SEQUENCE_TOKENS, 2), ((0, 64),), -0.2, 0.2), 0.25, 1.0)
    placement = draw_placement(jax.random.fold_in(seeds[13], 71), 0)
    gate_weight = scatter_about(seeds[10], (D, EXP_FLY * FF), D ** -0.5, 0.078125, ((0, 16), (1, 64)))
    up_weight = scatter_about(seeds[11], (D, EXP_FLY * FF), D ** -0.5, 0.078125, ((0, 16), (1, 64)))
    down_weight = scatter_about(seeds[12], (EXP_FLY * FF, D), FF ** -0.5, 0.0625, ((0, 64), (1, 16)))
    return {"queries": queries, "key_input": key_input, "value_input": value_input, "out_gate": out_gate, "log_decay": log_decay, "norm_gain": norm_gain, "features": features, "expert_ids": expert_ids, "route_weight": route_weight, "placement": placement, "gate_weight": gate_weight, "up_weight": up_weight, "down_weight": down_weight}


def slot_table(pairs, placement):
    flat = pairs.reshape(-1)
    match = (flat[:, None] == placement[None, :]).astype(jnp.int32)
    rank = jnp.cumsum(match, axis=0) - 1
    order = jnp.arange(CAP, dtype=jnp.int32)
    hits = (match[None, :, :] == 1) & (rank[None, :, :] == order[:, None, None])
    return jnp.transpose(hits, (2, 0, 1))

def attention_part(queries, key_input, value_input, out_gate, log_decay, norm_gain):
    blocks = queries.shape[0] // TOK_DEV
    shape = (blocks, TOK_DEV, HEADS, HEAD_DIM)
    query_b = queries.reshape(shape)
    key_b = key_input.reshape(shape)
    value_b = value_input.reshape(shape)
    decay_b = jnp.transpose(log_decay.reshape(HEADS, blocks, TOK_DEV), (1, 0, 2))
    lower = jnp.arange(TOK_DEV)[:, None] >= jnp.arange(TOK_DEV)[None, :]

    def step(state, item):
        query_c, key_c, value_c, decay_c = item
        query_f = query_c.astype(jnp.float32)
        key_f = key_c.astype(jnp.float32)
        value_f = value_c.astype(jnp.float32)
        cum = jnp.cumsum(decay_c, axis=1)
        scores = jnp.einsum('thd,shd->hts', query_f, key_f)
        spread = cum[:, :, None] - cum[:, None, :]
        weights = jnp.exp(jnp.where(lower[None], spread, -jnp.inf))
        probs = lax.optimization_barrier((scores * weights).astype(jnp.bfloat16)).astype(jnp.float32)
        intra = jnp.einsum('hts,shd->thd', probs, value_f)
        query_s = query_f * jnp.exp(cum).T[:, :, None]
        inter = jnp.einsum('thd,hde->the', query_s, state, precision=lax.Precision.HIGHEST)
        last = cum[:, -1]
        key_s = key_f * jnp.exp(last[:, None] - cum).T[:, :, None]
        local = jnp.einsum('thd,the->hde', key_s, value_f, precision=lax.Precision.HIGHEST)
        new_state = jnp.exp(last)[:, None, None] * state + local
        return (new_state, intra + inter)
    start = jnp.zeros((HEADS, HEAD_DIM, HEAD_DIM), jnp.float32)
    _, mixed = lax.scan(step, start, (query_b, key_b, value_b, decay_b))
    mixed = mixed.reshape(-1, HEADS, HEAD_DIM)
    power = lax.optimization_barrier(jnp.mean(mixed * mixed, axis=-1, keepdims=True))
    normed = mixed * lax.rsqrt(power + 1e-06)
    gates = jax.nn.sigmoid(out_gate.reshape(-1, HEADS, HEAD_DIM).astype(jnp.float32))
    result = normed * norm_gain.reshape(HEADS, HEAD_DIM) * gates
    return result.reshape(-1, HEADS * HEAD_DIM).astype(jnp.bfloat16)

def experts_part(features, expert_ids, route_weight, placement, gate_weight, up_weight, down_weight):
    blocks = features.shape[0] // TOK_DEV
    group = N_SEQ // EXP_FLY
    slice_width = FF // group
    hits = jax.vmap(lambda pairs: slot_table(pairs, placement))(expert_ids.reshape(blocks, TOK_DEV, 2))
    hits = hits.reshape(blocks, EXP_FLY, CAP, TOK_DEV, 2).astype(jnp.float32)
    pick = lax.optimization_barrier(jnp.sum(hits, axis=4))
    share = lax.optimization_barrier(jnp.sum(hits * route_weight.reshape(blocks, 1, 1, TOK_DEV, 2), axis=4))
    feats = features.reshape(blocks, TOK_DEV, D).astype(jnp.float32)
    rows = jnp.einsum('bjct,btd->jbcd', pick, feats).astype(jnp.bfloat16)

    def one_expert(item):
        chosen, index = item
        chosen = chosen.reshape(blocks * CAP, D)
        start = index * FF
        gate_cols = lax.dynamic_slice_in_dim(gate_weight, start, FF, 1)
        up_cols = lax.dynamic_slice_in_dim(up_weight, start, FF, 1)
        down_rows = lax.dynamic_slice_in_dim(down_weight, start, FF, 0)
        gate = jnp.dot(chosen, gate_cols, preferred_element_type=jnp.float32)
        up = jnp.dot(chosen, up_cols, preferred_element_type=jnp.float32)
        hidden = lax.optimization_barrier((jax.nn.silu(gate) * up).astype(jnp.bfloat16))
        hidden = hidden.astype(jnp.float32).reshape(-1, group, slice_width)
        pieces = jnp.einsum('rgf,gfd->rgd', hidden, down_rows.astype(jnp.float32).reshape(group, slice_width, D))
        pieces = lax.optimization_barrier(pieces.astype(jnp.bfloat16)).astype(jnp.float32)
        return lax.optimization_barrier(jnp.sum(pieces, axis=1)).reshape(blocks, CAP, D)
    outs = lax.map(one_expert, (rows, jnp.arange(EXP_FLY, dtype=jnp.int32)))
    mixed = jnp.einsum('bjct,jbcd->btd', share, outs, precision=lax.Precision.HIGHEST)
    return mixed.reshape(-1, D).astype(jnp.bfloat16)

def reference(queries, key_input, value_input, out_gate, log_decay, norm_gain, features, expert_ids, route_weight, placement, gate_weight, up_weight, down_weight):
    attention_out = attention_part(queries, key_input, value_input, out_gate, log_decay, norm_gain)
    moe_out = experts_part(features, expert_ids, route_weight, placement, gate_weight, up_weight, down_weight)
    return (attention_out, moe_out)
```

```python
import jax
import jax.numpy as jnp
from jax import lax
from jax.sharding import PartitionSpec as P

EXP_FLY = 4
CAP = 8


norm_eps = 1e-06


def slot_table(pairs, placement, slots):
    flat = pairs.reshape(-1)
    match = (flat[:, None] == placement[None, :]).astype(jnp.int32)
    rank = jnp.cumsum(match, axis=0) - 1
    order = jnp.arange(slots, dtype=jnp.int32)
    hits = (match[None, :, :] == 1) & (rank[None, :, :] == order[:, None, None])
    return jnp.transpose(hits, (2, 0, 1))


def split3(x):
    first = x.astype(jnp.bfloat16)
    rest = x - first.astype(jnp.float32)
    second = rest.astype(jnp.bfloat16)
    third = (rest - second.astype(jnp.float32)).astype(jnp.bfloat16)
    return jnp.stack([first, second, third], axis=-1)


def per_device(
    queries,
    key_input,
    value_input,
    out_gate,
    log_decay,
    norm_gain,
    features,
    expert_ids,
    route_weight,
    placement,
    gate_weight,
    up_weight,
    down_weight,
):
    seq_count = lax.axis_size("seq")
    head_count = lax.axis_size("head")
    group = seq_count // EXP_FLY
    tokens = queries.shape[0]
    heads_here = log_decay.shape[0]
    width = queries.shape[1] // heads_here
    feat = features.shape[1]
    ff = gate_weight.shape[1]
    half_cap = CAP // 2
    row_len = half_cap * feat
    query_h = queries.reshape(tokens, heads_here, width)
    key_h = key_input.reshape(tokens, heads_here, width)
    value_h = value_input.reshape(tokens, heads_here, width)

    decay_sum = jnp.cumsum(log_decay, axis=1)
    last = decay_sum[:, -1]
    key_scaled = key_h.astype(jnp.float32) * jnp.exp(last[:, None] - decay_sum).T[:, :, None]
    local_state = jnp.einsum(
        "thd,the->hde", key_scaled, value_h.astype(jnp.float32), precision=lax.Precision.HIGHEST
    )
    state_piece = local_state.astype(jnp.bfloat16).reshape(seq_count, -1)
    piece_len = state_piece.shape[1]
    log_piece = jnp.repeat(split3(last), seq_count // heads_here, axis=0)
    log_piece = jnp.pad(log_piece, ((0, 0), (0, 125)))

    hits = slot_table(expert_ids, placement, CAP).reshape(EXP_FLY, CAP, tokens, 2)
    pick = jnp.sum(hits.astype(jnp.int32), axis=3).astype(jnp.bfloat16)
    share = jnp.sum(hits.astype(jnp.float32) * route_weight[None, None, :, :], axis=3)
    outgoing = jnp.einsum("jct,td->jcd", pick, features, preferred_element_type=jnp.float32).astype(
        jnp.bfloat16
    )
    fanned = jnp.broadcast_to(
        outgoing.reshape(EXP_FLY, 1, 2, row_len), (EXP_FLY, group // 2, 2, row_len)
    ).reshape(seq_count, row_len)

    arrived = lax.all_to_all(
        jnp.concatenate([fanned, state_piece, log_piece], axis=1),
        "seq",
        split_axis=0,
        concat_axis=0,
        tiled=True,
    )
    swap = [(i, i ^ 1) for i in range(seq_count)]
    own_rows = arrived[:, :row_len].reshape(seq_count * half_cap, feat)
    other_rows = lax.ppermute(own_rows, "seq", swap)

    logs = jnp.sum(
        arrived[:, row_len + piece_len : row_len + piece_len + 3].astype(jnp.float32), axis=1
    )
    at = jnp.arange(seq_count)
    later = jnp.where(at[None, :] > at[:, None], logs[None, :], 0.0)
    before = (at[None, :] < at[:, None]).astype(jnp.float32)
    spans = jnp.einsum("bu,cu->bc", before, later, precision=lax.Precision.HIGHEST)
    mix = jnp.where(at[None, :] < at[:, None], jnp.exp(spans), 0.0)
    pieces_in = arrived[:, row_len : row_len + piece_len].astype(jnp.float32)
    prefix_piece = jnp.dot(mix, pieces_in, precision=lax.Precision.HIGHEST).astype(jnp.bfloat16)

    slot_rows = jnp.concatenate([own_rows, other_rows], axis=0)
    both_weight = jnp.concatenate([gate_weight, up_weight], axis=1)
    gate_up = jnp.dot(slot_rows, both_weight, preferred_element_type=jnp.float32).astype(
        jnp.bfloat16
    )
    rows = slot_rows.shape[0]
    parts = lax.all_to_all(
        gate_up.reshape(head_count, rows // head_count, 2 * ff),
        "head",
        split_axis=0,
        concat_axis=0,
        tiled=True,
    )
    summed = jnp.sum(parts.astype(jnp.float32), axis=0)
    hidden_part = (jax.nn.silu(summed[:, :ff]) * summed[:, ff:]).astype(jnp.bfloat16)
    hidden = lax.all_to_all(
        jnp.broadcast_to(hidden_part[None], (head_count,) + hidden_part.shape),
        "head",
        split_axis=0,
        concat_axis=0,
        tiled=True,
    ).reshape(rows, ff)
    partial_value = jnp.dot(hidden, down_weight, preferred_element_type=jnp.float32).astype(
        jnp.bfloat16
    )
    pair = lax.ppermute(partial_value[rows // 2 :], "seq", swap)
    piece = (partial_value[: rows // 2].astype(jnp.float32) + pair.astype(jnp.float32)).astype(
        jnp.bfloat16
    )
    returned = lax.all_to_all(
        jnp.concatenate([piece.reshape(seq_count, row_len), prefix_piece], axis=1),
        "seq",
        split_axis=0,
        concat_axis=0,
        tiled=True,
    )
    expert_out = jnp.sum(
        returned[:, :row_len].reshape(EXP_FLY, group // 2, CAP, feat).astype(jnp.float32), axis=1
    )
    moe_out = jnp.einsum("jct,jcd->td", share, expert_out, precision=lax.Precision.HIGHEST).astype(
        jnp.bfloat16
    )
    state_in = returned[:, row_len:].reshape(heads_here, width, width).astype(jnp.float32)

    scores = jnp.einsum("thd,shd->hts", query_h, key_h, preferred_element_type=jnp.float32)
    lower = jnp.arange(tokens)[:, None] >= jnp.arange(tokens)[None, :]
    spread = decay_sum[:, :, None] - decay_sum[:, None, :]
    weights = jnp.exp(jnp.where(lower[None], spread, -jnp.inf))
    probs = (scores * weights).astype(jnp.bfloat16)
    intra = jnp.einsum("hts,shd->thd", probs, value_h, preferred_element_type=jnp.float32)
    query_scaled = query_h.astype(jnp.float32) * jnp.exp(decay_sum).T[:, :, None]
    inter = jnp.einsum("thd,hde->the", query_scaled, state_in, precision=lax.Precision.HIGHEST)
    mixed = intra + inter
    power = jnp.mean(mixed * mixed, axis=-1, keepdims=True)
    normed = mixed * lax.rsqrt(power + norm_eps)
    gates = jax.nn.sigmoid(out_gate.reshape(tokens, heads_here, width).astype(jnp.float32))
    attention_out = (
        (normed * norm_gain.reshape(heads_here, width) * gates)
        .reshape(tokens, -1)
        .astype(jnp.bfloat16)
    )
    return (attention_out, moe_out)


def solution(mesh):
    placed = (
        P("seq", "head"),
        P("seq", "head"),
        P("seq", "head"),
        P("seq", "head"),
        P("head", "seq"),
        P("head"),
        P("seq", "head"),
        P("seq", None),
        P("seq", None),
        P(),
        P("head", "seq"),
        P("head", "seq"),
        P("seq", "head"),
    )
    return jax.shard_map(
        per_device,
        mesh=mesh,
        in_specs=placed,
        out_specs=(P("seq", "head"), P("seq", "head")),
        check_vma=False,
    )
```

```python
import jax
import jax.numpy as jnp
from jax import lax
from jax.sharding import PartitionSpec as P

EXP_FLY = 4
CAP = 8


norm_eps = 1e-06


def slot_table(pairs, placement, slots):
    flat = pairs.reshape(-1)
    match = (flat[:, None] == placement[None, :]).astype(jnp.int32)
    rank = jnp.cumsum(match, axis=0) - 1
    order = jnp.arange(slots, dtype=jnp.int32)
    hits = (match[None, :, :] == 1) & (rank[None, :, :] == order[:, None, None])
    return jnp.transpose(hits, (2, 0, 1))


def split3(x):
    first = x.astype(jnp.bfloat16)
    rest = x - first.astype(jnp.float32)
    second = rest.astype(jnp.bfloat16)
    third = (rest - second.astype(jnp.float32)).astype(jnp.bfloat16)
    return jnp.stack([first, second, third], axis=-1)


def per_device(
    queries,
    key_input,
    value_input,
    out_gate,
    log_decay,
    norm_gain,
    features,
    expert_ids,
    route_weight,
    placement,
    gate_weight,
    up_weight,
    down_weight,
):
    seq_count = lax.axis_size("seq")
    head_count = lax.axis_size("head")
    group = seq_count // EXP_FLY
    tokens = queries.shape[0]
    heads_here = log_decay.shape[0]
    width = queries.shape[1] // heads_here
    feat = features.shape[1]
    ff = gate_weight.shape[1]
    half_cap = CAP // 2
    row_len = half_cap * feat
    query_h = queries.reshape(tokens, heads_here, width)
    key_h = key_input.reshape(tokens, heads_here, width)
    value_h = value_input.reshape(tokens, heads_here, width)

    decay_sum = jnp.cumsum(log_decay, axis=1)
    last = decay_sum[:, -1]
    key_scaled = key_h.astype(jnp.float32) * jnp.exp(last[:, None] - decay_sum).T[:, :, None]
    local_state = jnp.einsum(
        "thd,the->hde", key_scaled, value_h.astype(jnp.float32), precision=lax.Precision.HIGHEST
    )
    state_piece = local_state.astype(jnp.bfloat16).reshape(seq_count, -1)
    piece_len = state_piece.shape[1]
    log_piece = jnp.repeat(split3(last), seq_count // heads_here, axis=0)
    log_piece = jnp.pad(log_piece, ((0, 0), (0, 125)))
    swap = [(i, i ^ 1) for i in range(seq_count)]
    other_gate = lax.ppermute(gate_weight, "seq", swap)
    other_up = lax.ppermute(up_weight, "seq", swap)
    other_down = lax.ppermute(down_weight, "seq", swap)

    hits = slot_table(expert_ids, placement, CAP).reshape(EXP_FLY, CAP, tokens, 2)
    pick = jnp.sum(hits.astype(jnp.int32), axis=3).astype(jnp.bfloat16)
    share = jnp.sum(hits.astype(jnp.float32) * route_weight[None, None, :, :], axis=3)
    outgoing = jnp.einsum("jct,td->jcd", pick, features, preferred_element_type=jnp.float32).astype(
        jnp.bfloat16
    )
    fanned = jnp.broadcast_to(
        outgoing.reshape(EXP_FLY, 1, 2, row_len), (EXP_FLY, group // 2, 2, row_len)
    ).reshape(seq_count, row_len)

    arrived = lax.all_to_all(
        jnp.concatenate([fanned, state_piece, log_piece], axis=1),
        "seq",
        split_axis=0,
        concat_axis=0,
        tiled=True,
    )
    slot_rows = arrived[:, :row_len].reshape(seq_count * half_cap, feat)
    arrived = arrived[:, row_len:]

    logs = jnp.sum(arrived[:, piece_len : piece_len + 3].astype(jnp.float32), axis=1)
    at = jnp.arange(seq_count)
    later = jnp.where(at[None, :] > at[:, None], logs[None, :], 0.0)
    before = (at[None, :] < at[:, None]).astype(jnp.float32)
    spans = jnp.einsum("bu,cu->bc", before, later, precision=lax.Precision.HIGHEST)
    mix = jnp.where(at[None, :] < at[:, None], jnp.exp(spans), 0.0)
    pieces_in = arrived[:, :piece_len].astype(jnp.float32)
    prefix_piece = jnp.dot(mix, pieces_in, precision=lax.Precision.HIGHEST).astype(
        jnp.bfloat16
    )
    both_weight = jnp.concatenate([gate_weight, other_gate, up_weight, other_up], axis=1)
    gate_up = jnp.dot(slot_rows, both_weight, preferred_element_type=jnp.float32).astype(
        jnp.bfloat16
    )
    rows = slot_rows.shape[0]
    parts = lax.all_to_all(
        gate_up.reshape(head_count, rows // head_count, 4 * ff),
        "head",
        split_axis=0,
        concat_axis=0,
        tiled=True,
    )
    summed = jnp.sum(parts.astype(jnp.float32), axis=0)
    hidden_part = (jax.nn.silu(summed[:, : 2 * ff]) * summed[:, 2 * ff :]).astype(jnp.bfloat16)
    hidden = lax.all_to_all(
        jnp.broadcast_to(hidden_part[None], (head_count,) + hidden_part.shape),
        "head",
        split_axis=0,
        concat_axis=0,
        tiled=True,
    ).reshape(rows, 2 * ff)
    piece = jnp.dot(
        hidden,
        jnp.concatenate([down_weight, other_down], axis=0),
        preferred_element_type=jnp.float32,
    ).astype(jnp.bfloat16)
    returned = lax.all_to_all(
        jnp.concatenate([piece.reshape(seq_count, row_len), prefix_piece], axis=1),
        "seq",
        split_axis=0,
        concat_axis=0,
        tiled=True,
    )
    expert_out = jnp.sum(
        returned[:, :row_len].reshape(EXP_FLY, group // 2, CAP, feat).astype(jnp.float32), axis=1
    )
    moe_out = jnp.einsum("jct,jcd->td", share, expert_out, precision=lax.Precision.HIGHEST).astype(
        jnp.bfloat16
    )
    state_in = returned[:, row_len:].reshape(heads_here, width, width).astype(jnp.float32)

    scores = jnp.einsum("thd,shd->hts", query_h, key_h, preferred_element_type=jnp.float32)
    lower = jnp.arange(tokens)[:, None] >= jnp.arange(tokens)[None, :]
    spread = decay_sum[:, :, None] - decay_sum[:, None, :]
    weights = jnp.exp(jnp.where(lower[None], spread, -jnp.inf))
    probs = (scores * weights).astype(jnp.bfloat16)
    intra = jnp.einsum("hts,shd->thd", probs, value_h, preferred_element_type=jnp.float32)
    query_scaled = query_h.astype(jnp.float32) * jnp.exp(decay_sum).T[:, :, None]
    inter = jnp.einsum("thd,hde->the", query_scaled, state_in, precision=lax.Precision.HIGHEST)
    mixed = intra + inter
    power = jnp.mean(mixed * mixed, axis=-1, keepdims=True)
    normed = mixed * lax.rsqrt(power + norm_eps)
    gates = jax.nn.sigmoid(out_gate.reshape(tokens, heads_here, width).astype(jnp.float32))
    attention_out = (
        (normed * norm_gain.reshape(heads_here, width) * gates)
        .reshape(tokens, -1)
        .astype(jnp.bfloat16)
    )
    return (attention_out, moe_out)


def solution(mesh):
    placed = (
        P("seq", "head"),
        P("seq", "head"),
        P("seq", "head"),
        P("seq", "head"),
        P("head", "seq"),
        P("head"),
        P("seq", "head"),
        P("seq", None),
        P("seq", None),
        P(),
        P("head", "seq"),
        P("head", "seq"),
        P("seq", "head"),
    )

    return jax.shard_map(
        per_device,
        mesh=mesh,
        in_specs=placed,
        out_specs=(P("seq", "head"), P("seq", "head")),
        check_vma=False,
    )
```

```python
import jax
import jax.numpy as jnp
from jax import lax
from jax.experimental import pallas as pl
from jax.experimental.pallas import tpu as pltpu
from jax.sharding import PartitionSpec as P

EXP_FLY = 4
HIGHEST = lax.Precision.HIGHEST
INTERPRET = False


norm_eps = 1e-06


def dot(a, b, dims, precision=None):
    return lax.dot_general(
        a, b, (dims, ((), ())), precision=precision, preferred_element_type=jnp.float32
    )


NN = ((1,), (0,))
NT = ((1,), (1,))
TN = ((0,), (0,))


def iota(shape, axis):
    return lax.broadcasted_iota(jnp.int32, shape, axis)


def two_parts(x):
    high = x.astype(jnp.bfloat16)
    return high, (x - high.astype(jnp.float32)).astype(jnp.bfloat16)


def picks(place_ref, ids, block_rows, tokens):
    q = iota((block_rows, tokens), 0)
    per_expert = block_rows // EXP_FLY
    wanted = jnp.zeros((block_rows, tokens), jnp.int32)
    for j in range(EXP_FLY):
        here = (q >= j * per_expert) & (q < (j + 1) * per_expert)
        wanted = jnp.where(here, place_ref[j], wanted)
    first = ids[0:1, :] == wanted
    second = ids[1:2, :] == wanted
    match = jnp.where(first | second, 1.0, 0.0).astype(jnp.bfloat16)
    upto = jnp.where(iota((tokens, tokens), 0) <= iota((tokens, tokens), 1), 1.0, 0.0)
    count = dot(match, upto.astype(jnp.bfloat16), NN)
    slot = (2 * (q & 3)).astype(jnp.float32)
    found = match.astype(jnp.float32) > 0.5
    return found & (count == slot + 1.0), found & (count == slot + 2.0), first


def pre_kernel(place_ref, key_ref, value_ref, decay_ref, feat_ref, ids_ref, out_ref):
    tokens, feat = feat_ref.shape
    heads = decay_ref.shape[0]
    width = key_ref.shape[1] // heads
    block_rows = out_ref.shape[0]
    per_head = block_rows // heads
    chunks = width // per_head
    decay = decay_ref[...]
    after = jnp.where(iota((tokens, tokens), 1) > iota((tokens, tokens), 0), 1.0, 0.0)
    rest = dot(after, decay, NT, HIGHEST)
    pick_a, pick_b, _ = picks(place_ref, ids_ref[...], block_rows, tokens)
    features = feat_ref[...]
    for at, pick in ((0, pick_a), (feat, pick_b)):
        one_hot = jnp.where(pick, 1.0, 0.0).astype(jnp.bfloat16)
        out_ref[:, at : at + feat] = dot(one_hot, features, NN).astype(jnp.bfloat16)
    start = 2 * feat
    logs = jnp.zeros((block_rows, 64), jnp.float32)
    q = iota((block_rows, 64), 0)
    for h in range(heads):
        cols = slice(h * width, (h + 1) * width)
        value = value_ref[:, cols]
        high, low = two_parts(key_ref[:, cols].astype(jnp.float32) * jnp.exp(rest[:, h : h + 1]))
        state = dot(high, value, TN) + dot(low, value, TN)
        rows = slice(h * per_head, (h + 1) * per_head)
        for i in range(chunks):
            out_ref[rows, start + i * width : start + (i + 1) * width] = state[
                i * per_head : (i + 1) * per_head
            ].astype(jnp.bfloat16)
        total = jnp.sum(decay[h : h + 1, :], axis=1, keepdims=True)
        here = (q >= h * per_head) & (q < (h + 1) * per_head)
        logs = jnp.where(here, total, logs)
    high = logs.astype(jnp.bfloat16).astype(jnp.float32)
    mid = (logs - high).astype(jnp.bfloat16).astype(jnp.float32)
    lane = iota((block_rows, 64), 1)
    parts = jnp.where(lane == 0, high, jnp.where(lane == 1, mid, logs - high - mid))
    stop = start + chunks * width
    out_ref[:, stop : stop + 64] = jnp.where(lane < 3, parts, 0.0).astype(jnp.bfloat16)


def scan_kernel(piece_ref, log_ref, out_ref):
    n = out_ref.shape[0]
    logs = jnp.sum(log_ref[:, 0:3].astype(jnp.float32), axis=1, keepdims=True)
    row, col = iota((n, n), 0), iota((n, n), 1)
    row_block, col_block = row >> 1, col >> 1
    before = jnp.where((col_block < row_block) & ((col & 1) == 0), 1.0, 0.0)
    later = jnp.where(row_block > col_block, logs, 0.0)
    spans = dot(before, later, NN, HIGHEST)
    used = (col_block < row_block) & ((col & 1) == (row & 1))
    high, low = two_parts(jnp.where(used, jnp.exp(spans), 0.0))
    pieces = piece_ref[...]
    out_ref[...] = (dot(high, pieces, NN) + dot(low, pieces, NN)).astype(jnp.bfloat16)


def down_kernel(hidden_ref, own_ref, other_ref, state_ref, out_ref):
    half = out_ref.shape[0]
    ff, feat = own_ref.shape
    piece = dot(hidden_ref[:, :ff], own_ref[...], NN) + dot(hidden_ref[:, ff:], other_ref[...], NN)
    out_ref[:, :feat] = piece[:half].astype(jnp.bfloat16)
    out_ref[:, feat : 2 * feat] = piece[half:].astype(jnp.bfloat16)
    out_ref[:, 2 * feat :] = state_ref[...]


def side_kernel(
    place_ref,
    query_ref,
    key_ref,
    value_ref,
    gate_ref,
    decay_ref,
    gain_ref,
    ids_ref,
    route_ref,
    intra_ref,
    factor_ref,
    high_ref,
    low_ref,
    share_high_ref,
    share_low_ref,
):
    tokens = query_ref.shape[0]
    heads = decay_ref.shape[0]
    width = query_ref.shape[1] // heads
    block_rows = share_high_ref.shape[0] // 2
    decay = decay_ref[...]
    row, col = iota((tokens, tokens), 0), iota((tokens, tokens), 1)
    lower = row >= col
    cum_col = dot(jnp.where(lower, 1.0, 0.0), decay, NT, HIGHEST)
    cum_row = dot(decay, jnp.where(row <= col, 1.0, 0.0), NN, HIGHEST)
    for h in range(heads):
        cols = slice(h * width, (h + 1) * width)
        query = query_ref[:, cols]
        scores = dot(query, key_ref[:, cols], NT)
        spread = cum_col[:, h : h + 1] - cum_row[h : h + 1, :]
        weights = jnp.where(lower, jnp.exp(jnp.where(lower, spread, 0.0)), 0.0)
        intra_ref[:, cols] = dot((scores * weights).astype(jnp.bfloat16), value_ref[:, cols], NN)
        scaled = query.astype(jnp.float32) * jnp.exp(cum_col[:, h : h + 1])
        high_ref[:, cols], low_ref[:, cols] = two_parts(scaled)
    factor_ref[...] = gain_ref[...] / (1.0 + jnp.exp(-gate_ref[...].astype(jnp.float32)))
    pick_a, pick_b, first = picks(place_ref, ids_ref[...], block_rows, tokens)
    route = route_ref[...]
    weight = jnp.where(first, route[0:1, :], route[1:2, :])
    for at, pick in ((0, pick_a), (block_rows, pick_b)):
        rows = slice(at, at + block_rows)
        share_high_ref[rows, :], share_low_ref[rows, :] = two_parts(jnp.where(pick, weight, 0.0))


def post_kernel(
    back_ref,
    intra_ref,
    factor_ref,
    high_ref,
    low_ref,
    share_high_ref,
    share_low_ref,
    attention_ref,
    moe_ref,
):
    block_rows = back_ref.shape[0]
    feat = moe_ref.shape[1]
    total = None
    for at in range(2):
        rows = slice(at * block_rows, (at + 1) * block_rows)
        pieces = back_ref[:, at * feat : (at + 1) * feat]
        part = dot(share_high_ref[rows, :], pieces, TN) + dot(share_low_ref[rows, :], pieces, TN)
        total = part if total is None else total + part
    moe_ref[...] = total.astype(jnp.bfloat16)
    width = 128
    heads = attention_ref.shape[1] // width
    per_head = block_rows // heads
    chunks = width // per_head
    for h in range(heads):
        cols = slice(h * width, (h + 1) * width)
        rows = slice(h * per_head, (h + 1) * per_head)
        state = jnp.concatenate(
            [
                back_ref[rows, 2 * feat + i * width : 2 * feat + (i + 1) * width]
                for i in range(chunks)
            ],
            axis=0,
        )
        mixed = (
            intra_ref[:, cols]
            + dot(high_ref[:, cols], state, NN)
            + dot(low_ref[:, cols], state, NN)
        )
        power = jnp.sum(mixed * mixed, axis=1, keepdims=True) * (1.0 / width)
        attention_ref[:, cols] = (mixed * lax.rsqrt(power + norm_eps) * factor_ref[:, cols]).astype(
            jnp.bfloat16
        )


def call(kernel, outs, scalars, cost, *arrays):
    specs = [pl.BlockSpec(memory_space=pltpu.SMEM)] * scalars
    specs += [pl.BlockSpec(memory_space=pltpu.VMEM)] * (len(arrays) - scalars)
    out_specs = [pl.BlockSpec(memory_space=pltpu.VMEM)] * len(outs)
    out_shape = [jax.ShapeDtypeStruct(shape, kind) for shape, kind in outs]
    if len(outs) == 1:
        out_specs, out_shape = out_specs[0], out_shape[0]
    return pl.pallas_call(
        kernel,
        in_specs=specs,
        out_specs=out_specs,
        out_shape=out_shape,
        cost_estimate=pl.CostEstimate(flops=cost, bytes_accessed=cost // 256, transcendentals=0),
        interpret=INTERPRET,
    )(*arrays)


def per_device(
    queries,
    key_input,
    value_input,
    out_gate,
    log_decay,
    norm_gain,
    features,
    expert_ids,
    route_weight,
    placement,
    gate_weight,
    up_weight,
    down_weight,
):
    seq_count = lax.axis_size("seq")
    head_count = lax.axis_size("head")
    tokens = queries.shape[0]
    heads_here = log_decay.shape[0]
    width = queries.shape[1] // heads_here
    feat = features.shape[1]
    ff = gate_weight.shape[1]
    bf16, f32 = jnp.bfloat16, jnp.float32
    lines = 2 * seq_count
    state_len = heads_here * width * width // lines
    ids = expert_ids.T
    swap = [(i, i ^ 1) for i in range(seq_count)]

    outgoing = call(
        pre_kernel,
        [((lines, 2 * feat + state_len + 64), bf16)],
        1,
        2**28,
        placement,
        key_input,
        value_input,
        log_decay,
        features,
        ids,
    )
    other_gate = lax.ppermute(gate_weight, "seq", swap)
    other_up = lax.ppermute(up_weight, "seq", swap)
    other_down = lax.ppermute(down_weight, "seq", swap)
    arrived = lax.all_to_all(
        outgoing.reshape(seq_count, 2, -1), "seq", split_axis=0, concat_axis=0, tiled=True
    ).reshape(lines, -1)

    slot_rows = jnp.concatenate([arrived[:, :feat], arrived[:, feat : 2 * feat]], axis=0)
    both_weight = jnp.concatenate([gate_weight, other_gate, up_weight, other_up], axis=1)
    gate_up = jnp.dot(slot_rows, both_weight, preferred_element_type=f32).astype(bf16)
    rows = slot_rows.shape[0]
    parts = lax.all_to_all(
        gate_up.reshape(head_count, rows // head_count, 4 * ff),
        "head",
        split_axis=0,
        concat_axis=0,
        tiled=True,
    )
    prefix_piece = call(
        scan_kernel,
        [((lines, state_len), bf16)],
        0,
        2**26,
        arrived[:, 2 * feat : 2 * feat + state_len],
        arrived[:, 2 * feat + state_len :],
    )
    summed = jnp.sum(parts.astype(f32), axis=0)
    hidden_part = (jax.nn.silu(summed[:, : 2 * ff]) * summed[:, 2 * ff :]).astype(bf16)
    hidden = lax.all_to_all(
        jnp.broadcast_to(hidden_part[None], (head_count,) + hidden_part.shape),
        "head",
        split_axis=0,
        concat_axis=0,
        tiled=True,
    ).reshape(rows, 2 * ff)
    leaving = call(
        down_kernel,
        [((lines, 2 * feat + state_len), bf16)],
        0,
        2**28,
        hidden,
        down_weight,
        other_down,
        prefix_piece,
    )
    returned = lax.all_to_all(
        leaving.reshape(seq_count, 2, -1), "seq", split_axis=0, concat_axis=0, tiled=True
    ).reshape(lines, -1)
    side = call(
        side_kernel,
        [
            ((tokens, heads_here * width), f32),
            ((tokens, heads_here * width), f32),
            ((tokens, heads_here * width), bf16),
            ((tokens, heads_here * width), bf16),
            ((2 * lines, tokens), bf16),
            ((2 * lines, tokens), bf16),
        ],
        1,
        2**29,
        placement,
        queries,
        key_input,
        value_input,
        out_gate,
        log_decay,
        norm_gain.reshape(1, -1),
        ids,
        route_weight.T,
    )
    attention_out, moe_out = call(
        post_kernel,
        [((tokens, heads_here * width), bf16), ((tokens, feat), bf16)],
        0,
        2**28,
        returned,
        *side,
    )
    return (attention_out, moe_out)


def solution(mesh):
    placed = (
        P("seq", "head"),
        P("seq", "head"),
        P("seq", "head"),
        P("seq", "head"),
        P("head", "seq"),
        P("head"),
        P("seq", "head"),
        P("seq", None),
        P("seq", None),
        P(),
        P("head", "seq"),
        P("head", "seq"),
        P("seq", "head"),
    )

    return jax.shard_map(
        per_device,
        mesh=mesh,
        in_specs=placed,
        out_specs=(P("seq", "head"), P("seq", "head")),
        check_vma=False,
    )
```

```python
import jax
import jax.numpy as jnp
from jax import lax
from jax.experimental import pallas as pl
from jax.experimental.pallas import tpu as pltpu
from jax.sharding import PartitionSpec as P

EXP_FLY = 4
HIGHEST = lax.Precision.HIGHEST
INTERPRET = False


norm_eps = 1e-06


def dot(a, b, dims, precision=None):
    return lax.dot_general(
        a, b, (dims, ((), ())), precision=precision, preferred_element_type=jnp.float32
    )


NN = ((1,), (0,))
NT = ((1,), (1,))
TN = ((0,), (0,))


def iota(shape, axis):
    return lax.broadcasted_iota(jnp.int32, shape, axis)


def two_parts(x):
    high = x.astype(jnp.bfloat16)
    return high, (x - high.astype(jnp.float32)).astype(jnp.bfloat16)


def picks(place_ref, ids, block_rows, tokens):
    q = iota((block_rows, tokens), 0)
    per_expert = block_rows // EXP_FLY
    wanted = jnp.zeros((block_rows, tokens), jnp.int32)
    for j in range(EXP_FLY):
        here = (q >= j * per_expert) & (q < (j + 1) * per_expert)
        wanted = jnp.where(here, place_ref[j], wanted)
    first = ids[0:1, :] == wanted
    second = ids[1:2, :] == wanted
    match = jnp.where(first | second, 1.0, 0.0).astype(jnp.bfloat16)
    upto = jnp.where(iota((tokens, tokens), 0) <= iota((tokens, tokens), 1), 1.0, 0.0)
    count = dot(match, upto.astype(jnp.bfloat16), NN)
    slot = (2 * (q & 2) + ((q & 4) >> 1) + (q & 1)).astype(jnp.float32)
    return (match.astype(jnp.float32) > 0.5) & (count == slot + 1.0), first


def in_pairs(x):
    return x.reshape(x.shape[0] // 2, 2, x.shape[1]).astype(jnp.bfloat16)


def pre_kernel(place_ref, key_ref, value_ref, decay_ref, feat_ref, ids_ref, out_ref):
    tokens, feat = feat_ref.shape
    heads = decay_ref.shape[0]
    width = key_ref.shape[1] // heads
    block_rows = 2 * out_ref.shape[0]
    per_head = block_rows // heads
    chunks = width // per_head
    decay = decay_ref[...]
    after = jnp.where(iota((tokens, tokens), 1) > iota((tokens, tokens), 0), 1.0, 0.0)
    rest = dot(after, decay, NT, HIGHEST)
    pick, _ = picks(place_ref, ids_ref[...], block_rows, tokens)
    one_hot = jnp.where(pick, 1.0, 0.0).astype(jnp.bfloat16)
    out_ref[:, :, :feat] = in_pairs(dot(one_hot, feat_ref[...], NN))
    start = feat
    logs = jnp.zeros((block_rows, 64), jnp.float32)
    q = iota((block_rows, 64), 0)
    for h in range(heads):
        cols = slice(h * width, (h + 1) * width)
        value = value_ref[:, cols]
        high, low = two_parts(key_ref[:, cols].astype(jnp.float32) * jnp.exp(rest[:, h : h + 1]))
        state = dot(high, value, TN) + dot(low, value, TN)
        rows = slice(h * per_head // 2, (h + 1) * per_head // 2)
        for i in range(chunks):
            out_ref[rows, :, start + i * width : start + (i + 1) * width] = in_pairs(
                state[i * per_head : (i + 1) * per_head]
            )
        total = jnp.sum(decay[h : h + 1, :], axis=1, keepdims=True)
        here = (q >= h * per_head) & (q < (h + 1) * per_head)
        logs = jnp.where(here, total, logs)
    high = logs.astype(jnp.bfloat16).astype(jnp.float32)
    mid = (logs - high).astype(jnp.bfloat16).astype(jnp.float32)
    lane = iota((block_rows, 64), 1)
    parts = jnp.where(lane == 0, high, jnp.where(lane == 1, mid, logs - high - mid))
    stop = start + chunks * width
    out_ref[:, :, stop : stop + 64] = in_pairs(jnp.where(lane < 3, parts, 0.0))


def scan_kernel(piece_ref, log_ref, out_ref):
    n = out_ref.shape[0]
    logs = jnp.sum(log_ref[:, 0:3].astype(jnp.float32), axis=1, keepdims=True)
    row, col = iota((n, n), 0), iota((n, n), 1)
    row_block, col_block = row >> 1, col >> 1
    before = jnp.where((col_block < row_block) & ((col & 1) == 0), 1.0, 0.0)
    later = jnp.where(row_block > col_block, logs, 0.0)
    spans = dot(before, later, NN, HIGHEST)
    used = (col_block < row_block) & ((col & 1) == (row & 1))
    high, low = two_parts(jnp.where(used, jnp.exp(spans), 0.0))
    pieces = piece_ref[...]
    out_ref[...] = (dot(high, pieces, NN) + dot(low, pieces, NN)).astype(jnp.bfloat16)


def side_kernel(
    place_ref,
    query_ref,
    key_ref,
    value_ref,
    gate_ref,
    decay_ref,
    gain_ref,
    ids_ref,
    route_ref,
    intra_ref,
    factor_ref,
    high_ref,
    low_ref,
    share_high_ref,
    share_low_ref,
):
    tokens = query_ref.shape[0]
    heads = decay_ref.shape[0]
    width = query_ref.shape[1] // heads
    block_rows = share_high_ref.shape[0]
    decay = decay_ref[...]
    row, col = iota((tokens, tokens), 0), iota((tokens, tokens), 1)
    lower = row >= col
    cum_col = dot(jnp.where(lower, 1.0, 0.0), decay, NT, HIGHEST)
    cum_row = dot(decay, jnp.where(row <= col, 1.0, 0.0), NN, HIGHEST)
    for h in range(heads):
        cols = slice(h * width, (h + 1) * width)
        query = query_ref[:, cols]
        scores = dot(query, key_ref[:, cols], NT)
        spread = cum_col[:, h : h + 1] - cum_row[h : h + 1, :]
        weights = jnp.where(lower, jnp.exp(jnp.where(lower, spread, 0.0)), 0.0)
        intra_ref[:, cols] = dot((scores * weights).astype(jnp.bfloat16), value_ref[:, cols], NN)
        scaled = query.astype(jnp.float32) * jnp.exp(cum_col[:, h : h + 1])
        high_ref[:, cols], low_ref[:, cols] = two_parts(scaled)
    factor_ref[...] = gain_ref[...] / (1.0 + jnp.exp(-gate_ref[...].astype(jnp.float32)))
    pick, first = picks(place_ref, ids_ref[...], block_rows, tokens)
    route = route_ref[...]
    weight = jnp.where(first, route[0:1, :], route[1:2, :])
    share_high_ref[...], share_low_ref[...] = two_parts(jnp.where(pick, weight, 0.0))


def post_kernel(
    back_ref,
    intra_ref,
    factor_ref,
    high_ref,
    low_ref,
    share_high_ref,
    share_low_ref,
    attention_ref,
    moe_ref,
):
    block_rows = back_ref.shape[0]
    feat = moe_ref.shape[1]
    pieces = back_ref[:, :feat]
    total = dot(share_high_ref[...], pieces, TN) + dot(share_low_ref[...], pieces, TN)
    moe_ref[...] = total.astype(jnp.bfloat16)
    width = 128
    heads = attention_ref.shape[1] // width
    per_head = block_rows // heads
    chunks = width // per_head
    for h in range(heads):
        cols = slice(h * width, (h + 1) * width)
        rows = slice(h * per_head, (h + 1) * per_head)
        state = jnp.concatenate(
            [
                back_ref[rows, feat + i * width : feat + (i + 1) * width]
                for i in range(chunks)
            ],
            axis=0,
        )
        mixed = (
            intra_ref[:, cols]
            + dot(high_ref[:, cols], state, NN)
            + dot(low_ref[:, cols], state, NN)
        )
        power = jnp.sum(mixed * mixed, axis=1, keepdims=True) * (1.0 / width)
        attention_ref[:, cols] = (mixed * lax.rsqrt(power + norm_eps) * factor_ref[:, cols]).astype(
            jnp.bfloat16
        )


def call(kernel, outs, scalars, cost, *arrays):
    specs = [pl.BlockSpec(memory_space=pltpu.SMEM)] * scalars
    specs += [pl.BlockSpec(memory_space=pltpu.VMEM)] * (len(arrays) - scalars)
    out_specs = [pl.BlockSpec(memory_space=pltpu.VMEM)] * len(outs)
    out_shape = [jax.ShapeDtypeStruct(shape, kind) for shape, kind in outs]
    if len(outs) == 1:
        out_specs, out_shape = out_specs[0], out_shape[0]
    return pl.pallas_call(
        kernel,
        in_specs=specs,
        out_specs=out_specs,
        out_shape=out_shape,
        cost_estimate=pl.CostEstimate(flops=cost, bytes_accessed=cost // 256, transcendentals=0),
        interpret=INTERPRET,
    )(*arrays)


def per_device(
    queries,
    key_input,
    value_input,
    out_gate,
    log_decay,
    norm_gain,
    features,
    expert_ids,
    route_weight,
    placement,
    gate_weight,
    up_weight,
    down_weight,
):
    seq_count = lax.axis_size("seq")
    head_count = lax.axis_size("head")
    tokens = queries.shape[0]
    heads_here = log_decay.shape[0]
    width = queries.shape[1] // heads_here
    feat = features.shape[1]
    ff = gate_weight.shape[1]
    bf16, f32 = jnp.bfloat16, jnp.float32
    lines = 2 * seq_count
    state_len = heads_here * width * width // lines
    ids = expert_ids.T
    swap = [(i, i ^ 1) for i in range(seq_count)]
    next_chip = [(i, i ^ 2) for i in range(seq_count)]

    outgoing = call(
        pre_kernel,
        [((seq_count, 2, feat + state_len + 64), bf16)],
        1,
        2**28,
        placement,
        key_input,
        value_input,
        log_decay,
        features,
        ids,
    )
    other_gate = lax.ppermute(gate_weight, "seq", swap)
    other_up = lax.ppermute(up_weight, "seq", swap)
    other_down = lax.ppermute(down_weight, "seq", swap)
    arrived = lax.all_to_all(
        outgoing, "seq", split_axis=0, concat_axis=0, tiled=True
    ).reshape(lines, -1)

    own_rows = arrived[:, :feat]
    near_rows = lax.ppermute(own_rows, "seq", next_chip)
    slot_rows = jnp.concatenate([own_rows, near_rows], axis=0)
    both_weight = jnp.concatenate([gate_weight, other_gate, up_weight, other_up], axis=1)
    gate_up = jnp.dot(slot_rows, both_weight, preferred_element_type=f32).astype(bf16)
    rows = slot_rows.shape[0]
    parts = lax.all_to_all(
        gate_up.reshape(head_count, rows // head_count, 4 * ff),
        "head",
        split_axis=0,
        concat_axis=0,
        tiled=True,
    )
    prefix_piece = call(
        scan_kernel,
        [((lines, state_len), bf16)],
        0,
        2**26,
        arrived[:, feat : feat + state_len],
        arrived[:, feat + state_len :],
    )
    summed = jnp.sum(parts.astype(f32), axis=0)
    hidden_part = (jax.nn.silu(summed[:, : 2 * ff]) * summed[:, 2 * ff :]).astype(bf16)
    hidden = lax.all_to_all(
        jnp.broadcast_to(hidden_part[None], (head_count,) + hidden_part.shape),
        "head",
        split_axis=0,
        concat_axis=0,
        tiled=True,
    ).reshape(rows, 2 * ff)
    piece = jnp.dot(
        hidden,
        jnp.concatenate([down_weight, other_down], axis=0),
        preferred_element_type=f32,
    ).astype(bf16)
    near_piece = lax.ppermute(piece[lines:], "seq", next_chip)
    piece = (piece[:lines].astype(f32) + near_piece.astype(f32)).astype(bf16)
    leaving = jnp.concatenate([piece, prefix_piece], axis=1)
    returned = lax.all_to_all(
        leaving.reshape(seq_count, 2, -1), "seq", split_axis=0, concat_axis=0, tiled=True
    ).reshape(lines, -1)
    side = call(
        side_kernel,
        [
            ((tokens, heads_here * width), f32),
            ((tokens, heads_here * width), f32),
            ((tokens, heads_here * width), bf16),
            ((tokens, heads_here * width), bf16),
            ((lines, tokens), bf16),
            ((lines, tokens), bf16),
        ],
        1,
        2**29,
        placement,
        queries,
        key_input,
        value_input,
        out_gate,
        log_decay,
        norm_gain.reshape(1, -1),
        ids,
        route_weight.T,
    )
    attention_out, moe_out = call(
        post_kernel,
        [((tokens, heads_here * width), bf16), ((tokens, feat), bf16)],
        0,
        2**28,
        returned,
        *side,
    )
    return (attention_out, moe_out)


def solution(mesh):
    placed = (
        P("seq", "head"),
        P("seq", "head"),
        P("seq", "head"),
        P("seq", "head"),
        P("head", "seq"),
        P("head"),
        P("seq", "head"),
        P("seq", None),
        P("seq", None),
        P(),
        P("head", "seq"),
        P("head", "seq"),
        P("seq", "head"),
    )

    return jax.shard_map(
        per_device,
        mesh=mesh,
        in_specs=placed,
        out_specs=(P("seq", "head"), P("seq", "head")),
        check_vma=False,
    )
```

```python
import jax
import jax.numpy as jnp
from jax import lax
from jax.experimental import pallas as pl
from jax.experimental.pallas import tpu as pltpu
from jax.sharding import PartitionSpec as P

EXP_FLY = 4
HIGHEST = lax.Precision.HIGHEST
INTERPRET = False


norm_eps = 1e-06


def dot(a, b, dims, precision=None):
    return lax.dot_general(
        a, b, (dims, ((), ())), precision=precision, preferred_element_type=jnp.float32
    )


NN = ((1,), (0,))
NT = ((1,), (1,))
TN = ((0,), (0,))


def iota(shape, axis):
    return lax.broadcasted_iota(jnp.int32, shape, axis)


def two_parts(x):
    high = x.astype(jnp.bfloat16)
    return high, (x - high.astype(jnp.float32)).astype(jnp.bfloat16)


def picks(place_ref, ids, block_rows, tokens):
    q = iota((block_rows, tokens), 0)
    per_expert = block_rows // EXP_FLY
    wanted = jnp.zeros((block_rows, tokens), jnp.int32)
    for j in range(EXP_FLY):
        here = (q >= j * per_expert) & (q < (j + 1) * per_expert)
        wanted = jnp.where(here, place_ref[j], wanted)
    first = ids[0:1, :] == wanted
    second = ids[1:2, :] == wanted
    match = jnp.where(first | second, 1.0, 0.0).astype(jnp.bfloat16)
    upto = jnp.where(iota((tokens, tokens), 0) <= iota((tokens, tokens), 1), 1.0, 0.0)
    count = dot(match, upto.astype(jnp.bfloat16), NN)
    slot = (2 * (q & 2) + ((q & 4) >> 1) + (q & 1)).astype(jnp.float32)
    return (match.astype(jnp.float32) > 0.5) & (count == slot + 1.0), first


def in_pairs(x):
    return x.reshape(x.shape[0] // 2, 2, x.shape[1]).astype(jnp.bfloat16)


def pre_kernel(place_ref, key_ref, value_ref, decay_ref, feat_ref, ids_ref, out_ref):
    tokens, feat = feat_ref.shape
    heads = decay_ref.shape[0]
    width = key_ref.shape[1] // heads
    block_rows = 2 * out_ref.shape[0]
    per_head = block_rows // heads
    chunks = width // per_head
    decay = decay_ref[...]
    after = jnp.where(iota((tokens, tokens), 1) > iota((tokens, tokens), 0), 1.0, 0.0)
    rest = dot(after, decay, NT, HIGHEST)
    pick, _ = picks(place_ref, ids_ref[...], block_rows, tokens)
    one_hot = jnp.where(pick, 1.0, 0.0).astype(jnp.bfloat16)
    out_ref[:, :, :feat] = in_pairs(dot(one_hot, feat_ref[...], NN))
    start = feat
    logs = jnp.zeros((block_rows, 64), jnp.float32)
    q = iota((block_rows, 64), 0)
    for h in range(heads):
        cols = slice(h * width, (h + 1) * width)
        value = value_ref[:, cols]
        key = key_ref[:, cols].astype(jnp.float32) * jnp.exp(rest[:, h : h + 1])
        state = dot(key.astype(jnp.bfloat16), value, TN)
        rows = slice(h * per_head // 2, (h + 1) * per_head // 2)
        for i in range(chunks):
            out_ref[rows, :, start + i * width : start + (i + 1) * width] = in_pairs(
                state[i * per_head : (i + 1) * per_head]
            )
        total = jnp.sum(decay[h : h + 1, :], axis=1, keepdims=True)
        here = (q >= h * per_head) & (q < (h + 1) * per_head)
        logs = jnp.where(here, total, logs)
    high = logs.astype(jnp.bfloat16).astype(jnp.float32)
    mid = (logs - high).astype(jnp.bfloat16).astype(jnp.float32)
    lane = iota((block_rows, 64), 1)
    parts = jnp.where(lane == 0, high, jnp.where(lane == 1, mid, logs - high - mid))
    stop = start + chunks * width
    out_ref[:, :, stop : stop + 64] = in_pairs(jnp.where(lane < 3, parts, 0.0))


def flat(x):
    return x.astype(jnp.float32).reshape(2 * x.shape[0], x.shape[2]).astype(jnp.bfloat16)


def scan_kernel(piece_ref, log_ref, out_ref):
    n = 2 * out_ref.shape[0]
    feat = out_ref.shape[2] - piece_ref.shape[1]
    logs = jnp.sum(log_ref[:, 0:3].astype(jnp.float32), axis=1, keepdims=True)
    row, col = iota((n, n), 0), iota((n, n), 1)
    row_block, col_block = row >> 1, col >> 1
    before = jnp.where((col_block < row_block) & ((col & 1) == 0), 1.0, 0.0)
    later = jnp.where(row_block > col_block, logs, 0.0)
    spans = dot(before, later, NN, HIGHEST)
    used = (col_block < row_block) & ((col & 1) == (row & 1))
    high, low = two_parts(jnp.where(used, jnp.exp(spans), 0.0))
    pieces = piece_ref[...]
    out_ref[:, :, :feat] = jnp.zeros((n // 2, 2, feat), jnp.bfloat16)
    out_ref[:, :, feat:] = in_pairs(dot(high, pieces, NN) + dot(low, pieces, NN))


def side_kernel(
    place_ref,
    query_ref,
    key_ref,
    value_ref,
    gate_ref,
    decay_ref,
    gain_ref,
    ids_ref,
    route_ref,
    intra_ref,
    factor_ref,
    scaled_ref,
    share_high_ref,
    share_low_ref,
):
    tokens = query_ref.shape[0]
    heads = decay_ref.shape[0]
    width = query_ref.shape[1] // heads
    block_rows = share_high_ref.shape[0]
    decay = decay_ref[...]
    row, col = iota((tokens, tokens), 0), iota((tokens, tokens), 1)
    lower = row >= col
    cum_col = dot(jnp.where(lower, 1.0, 0.0), decay, NT, HIGHEST)
    cum_row = dot(decay, jnp.where(row <= col, 1.0, 0.0), NN, HIGHEST)
    for h in range(heads):
        cols = slice(h * width, (h + 1) * width)
        query = query_ref[:, cols]
        scores = dot(query, key_ref[:, cols], NT)
        spread = cum_col[:, h : h + 1] - cum_row[h : h + 1, :]
        weights = jnp.where(lower, jnp.exp(jnp.where(lower, spread, 0.0)), 0.0)
        intra_ref[:, cols] = dot((scores * weights).astype(jnp.bfloat16), value_ref[:, cols], NN)
        scaled = query.astype(jnp.float32) * jnp.exp(cum_col[:, h : h + 1])
        scaled_ref[:, cols] = scaled.astype(jnp.bfloat16)
    factor_ref[...] = gain_ref[...] / (1.0 + jnp.exp(-gate_ref[...].astype(jnp.float32)))
    pick, first = picks(place_ref, ids_ref[...], block_rows, tokens)
    route = route_ref[...]
    weight = jnp.where(first, route[0:1, :], route[1:2, :])
    share_high_ref[...], share_low_ref[...] = two_parts(jnp.where(pick, weight, 0.0))


def post_kernel(
    back_ref,
    intra_ref,
    factor_ref,
    scaled_ref,
    share_high_ref,
    share_low_ref,
    attention_ref,
    moe_ref,
):
    block_rows = 2 * back_ref.shape[0]
    feat = moe_ref.shape[1]
    pieces = flat(back_ref[:, :, :feat])
    total = dot(share_high_ref[...], pieces, TN) + dot(share_low_ref[...], pieces, TN)
    moe_ref[...] = total.astype(jnp.bfloat16)
    width = 128
    heads = attention_ref.shape[1] // width
    per_head = block_rows // heads
    chunks = width // per_head
    for h in range(heads):
        cols = slice(h * width, (h + 1) * width)
        rows = slice(h * per_head // 2, (h + 1) * per_head // 2)
        state = jnp.concatenate(
            [
                flat(back_ref[rows, :, feat + i * width : feat + (i + 1) * width])
                for i in range(chunks)
            ],
            axis=0,
        )
        mixed = intra_ref[:, cols] + dot(scaled_ref[:, cols], state, NN)
        power = jnp.sum(mixed * mixed, axis=1, keepdims=True) * (1.0 / width)
        attention_ref[:, cols] = (mixed * lax.rsqrt(power + norm_eps) * factor_ref[:, cols]).astype(
            jnp.bfloat16
        )


def call(kernel, outs, scalars, cost, *arrays):
    specs = [pl.BlockSpec(memory_space=pltpu.SMEM)] * scalars
    specs += [pl.BlockSpec(memory_space=pltpu.VMEM)] * (len(arrays) - scalars)
    out_specs = [pl.BlockSpec(memory_space=pltpu.VMEM)] * len(outs)
    out_shape = [jax.ShapeDtypeStruct(shape, kind) for shape, kind in outs]
    if len(outs) == 1:
        out_specs, out_shape = out_specs[0], out_shape[0]
    return pl.pallas_call(
        kernel,
        in_specs=specs,
        out_specs=out_specs,
        out_shape=out_shape,
        cost_estimate=pl.CostEstimate(flops=cost, bytes_accessed=cost // 256, transcendentals=0),
        interpret=INTERPRET,
    )(*arrays)


def per_device(
    queries,
    key_input,
    value_input,
    out_gate,
    log_decay,
    norm_gain,
    features,
    expert_ids,
    route_weight,
    placement,
    gate_weight,
    up_weight,
    down_weight,
):
    seq_count = lax.axis_size("seq")
    head_count = lax.axis_size("head")
    tokens = queries.shape[0]
    heads_here = log_decay.shape[0]
    width = queries.shape[1] // heads_here
    feat = features.shape[1]
    ff = gate_weight.shape[1]
    bf16, f32 = jnp.bfloat16, jnp.float32
    lines = 2 * seq_count
    state_len = heads_here * width * width // lines
    ids = expert_ids.T
    swap = [(i, i ^ 1) for i in range(seq_count)]
    next_chip = [(i, i ^ 2) for i in range(seq_count)]

    outgoing = call(
        pre_kernel,
        [((seq_count, 2, feat + state_len + 64), bf16)],
        1,
        2**28,
        placement,
        key_input,
        value_input,
        log_decay,
        features,
        ids,
    )
    other_gate = lax.ppermute(gate_weight, "seq", swap)
    other_up = lax.ppermute(up_weight, "seq", swap)
    other_down = lax.ppermute(down_weight, "seq", swap)
    arrived = lax.all_to_all(
        outgoing, "seq", split_axis=0, concat_axis=0, tiled=True
    ).reshape(lines, -1)

    own_rows = arrived[:, :feat]
    near_rows = lax.ppermute(own_rows, "seq", next_chip)
    slot_rows = jnp.concatenate([own_rows, near_rows], axis=0)
    both_weight = jnp.concatenate([gate_weight, other_gate, up_weight, other_up], axis=1)
    gate_up = jnp.dot(slot_rows, both_weight, preferred_element_type=f32).astype(bf16)
    rows = slot_rows.shape[0]
    parts = lax.all_to_all(
        gate_up.reshape(head_count, rows // head_count, 4 * ff),
        "head",
        split_axis=0,
        concat_axis=0,
        tiled=True,
    )
    prefix_piece = call(
        scan_kernel,
        [((seq_count, 2, feat + state_len), bf16)],
        0,
        2**26,
        arrived[:, feat : feat + state_len],
        arrived[:, feat + state_len :],
    )
    summed = jnp.sum(parts.astype(f32), axis=0)
    hidden_part = (jax.nn.silu(summed[:, : 2 * ff]) * summed[:, 2 * ff :]).astype(bf16)
    hidden = lax.all_to_all(
        jnp.broadcast_to(hidden_part[None], (head_count,) + hidden_part.shape),
        "head",
        split_axis=0,
        concat_axis=0,
        tiled=True,
    ).reshape(rows, 2 * ff)
    piece = jnp.dot(
        hidden,
        jnp.concatenate([down_weight, other_down], axis=0),
        preferred_element_type=f32,
    ).astype(bf16)
    near_piece = lax.ppermute(piece[lines:], "seq", next_chip)
    piece = (piece[:lines].astype(f32) + near_piece.astype(f32)).astype(bf16)
    leaving = lax.dynamic_update_slice(
        prefix_piece, piece.reshape(seq_count, 2, feat), (0, 0, 0)
    )
    returned = lax.all_to_all(
        leaving, "seq", split_axis=0, concat_axis=0, tiled=True
    )
    side = call(
        side_kernel,
        [
            ((tokens, heads_here * width), f32),
            ((tokens, heads_here * width), f32),
            ((tokens, heads_here * width), bf16),
            ((lines, tokens), bf16),
            ((lines, tokens), bf16),
        ],
        1,
        2**29,
        placement,
        queries,
        key_input,
        value_input,
        out_gate,
        log_decay,
        norm_gain.reshape(1, -1),
        ids,
        route_weight.T,
    )
    attention_out, moe_out = call(
        post_kernel,
        [((tokens, heads_here * width), bf16), ((tokens, feat), bf16)],
        0,
        2**28,
        returned,
        *side,
    )
    return (attention_out, moe_out)


def solution(mesh):
    placed = (
        P("seq", "head"),
        P("seq", "head"),
        P("seq", "head"),
        P("seq", "head"),
        P("head", "seq"),
        P("head"),
        P("seq", "head"),
        P("seq", None),
        P("seq", None),
        P(),
        P("head", "seq"),
        P("head", "seq"),
        P("seq", "head"),
    )

    return jax.shard_map(
        per_device,
        mesh=mesh,
        in_specs=placed,
        out_specs=(P("seq", "head"), P("seq", "head")),
        check_vma=False,
    )
```

```python
import jax
import jax.numpy as jnp
from jax import lax
from jax.experimental import pallas as pl
from jax.experimental.pallas import tpu as pltpu
from jax.sharding import PartitionSpec as P

EXP_FLY = 4
HIGHEST = lax.Precision.HIGHEST
INTERPRET = False


norm_eps = 1e-06


def dot(a, b, dims, precision=None):
    return lax.dot_general(
        a, b, (dims, ((), ())), precision=precision, preferred_element_type=jnp.float32
    )


NN = ((1,), (0,))
NT = ((1,), (1,))
TN = ((0,), (0,))


def iota(shape, axis):
    return lax.broadcasted_iota(jnp.int32, shape, axis)


def two_parts(x):
    high = x.astype(jnp.bfloat16)
    return high, (x - high.astype(jnp.float32)).astype(jnp.bfloat16)


def picks(place_ref, ids, block_rows, tokens):
    q = iota((block_rows, tokens), 0)
    per_expert = block_rows // EXP_FLY
    wanted = jnp.zeros((block_rows, tokens), jnp.int32)
    for j in range(EXP_FLY):
        here = (q >= j * per_expert) & (q < (j + 1) * per_expert)
        wanted = jnp.where(here, place_ref[j], wanted)
    first = ids[0:1, :] == wanted
    second = ids[1:2, :] == wanted
    match = jnp.where(first | second, 1.0, 0.0).astype(jnp.bfloat16)
    upto = jnp.where(iota((tokens, tokens), 0) <= iota((tokens, tokens), 1), 1.0, 0.0)
    count = dot(match, upto.astype(jnp.bfloat16), NN)
    slot = (2 * (q & 2) + ((q & 4) >> 1) + (q & 1)).astype(jnp.float32)
    return (match.astype(jnp.float32) > 0.5) & (count == slot + 1.0), first


def in_pairs(x):
    return x.reshape(x.shape[0] // 2, 2, x.shape[1]).astype(jnp.bfloat16)


def pre_kernel(place_ref, key_ref, value_ref, decay_ref, feat_ref, ids_ref, out_ref):
    tokens, feat = feat_ref.shape
    heads = decay_ref.shape[0]
    width = key_ref.shape[1] // heads
    block_rows = 2 * out_ref.shape[0]
    per_head = block_rows // heads
    chunks = width // per_head
    decay = decay_ref[...]
    after = jnp.where(iota((tokens, tokens), 1) > iota((tokens, tokens), 0), 1.0, 0.0)
    rest = dot(after, decay, NT, HIGHEST)
    pick, _ = picks(place_ref, ids_ref[...], block_rows, tokens)
    one_hot = jnp.where(pick, 1.0, 0.0).astype(jnp.bfloat16)
    out_ref[:, :, :feat] = in_pairs(dot(one_hot, feat_ref[...], NN))
    start = feat
    logs = jnp.zeros((block_rows, 64), jnp.float32)
    q = iota((block_rows, 64), 0)
    for h in range(heads):
        cols = slice(h * width, (h + 1) * width)
        value = value_ref[:, cols]
        key = key_ref[:, cols].astype(jnp.float32) * jnp.exp(rest[:, h : h + 1])
        state = dot(key.astype(jnp.bfloat16), value, TN)
        rows = slice(h * per_head // 2, (h + 1) * per_head // 2)
        for i in range(chunks):
            out_ref[rows, :, start + i * width : start + (i + 1) * width] = in_pairs(
                state[i * per_head : (i + 1) * per_head]
            )
        total = jnp.sum(decay[h : h + 1, :], axis=1, keepdims=True)
        here = (q >= h * per_head) & (q < (h + 1) * per_head)
        logs = jnp.where(here, total, logs)
    high = logs.astype(jnp.bfloat16).astype(jnp.float32)
    mid = (logs - high).astype(jnp.bfloat16).astype(jnp.float32)
    lane = iota((block_rows, 64), 1)
    parts = jnp.where(lane == 0, high, jnp.where(lane == 1, mid, logs - high - mid))
    stop = start + chunks * width
    out_ref[:, :, stop : stop + 64] = in_pairs(jnp.where(lane < 3, parts, 0.0))


def flat(x):
    return x.astype(jnp.float32).reshape(2 * x.shape[0], x.shape[2]).astype(jnp.bfloat16)


STATE = 4 * 128 * 128


def scan_kernel(arrived_ref, out_ref):
    n = 2 * out_ref.shape[0]
    end = out_ref.shape[2]
    feat = end - STATE // n
    logs = jnp.sum(arrived_ref[:, end : end + 3].astype(jnp.float32), axis=1, keepdims=True)
    row, col = iota((n, n), 0), iota((n, n), 1)
    row_block, col_block = row >> 1, col >> 1
    before = jnp.where((col_block < row_block) & ((col & 1) == 0), 1.0, 0.0)
    later = jnp.where(row_block > col_block, logs, 0.0)
    spans = dot(before, later, NN, HIGHEST)
    used = (col_block < row_block) & ((col & 1) == (row & 1))
    high, low = two_parts(jnp.where(used, jnp.exp(spans), 0.0))
    pieces = arrived_ref[:, feat:end]
    out_ref[:, :, :feat] = jnp.zeros((n // 2, 2, feat), jnp.bfloat16)
    out_ref[:, :, feat:] = in_pairs(dot(high, pieces, NN) + dot(low, pieces, NN))


def side_kernel(
    place_ref,
    query_ref,
    key_ref,
    value_ref,
    gate_ref,
    decay_ref,
    gain_ref,
    ids_ref,
    route_ref,
    intra_ref,
    factor_ref,
    scaled_ref,
    share_high_ref,
    share_low_ref,
):
    tokens = query_ref.shape[0]
    heads = decay_ref.shape[0]
    width = query_ref.shape[1] // heads
    block_rows = share_high_ref.shape[0]
    decay = decay_ref[...]
    row, col = iota((tokens, tokens), 0), iota((tokens, tokens), 1)
    lower = row >= col
    cum_col = dot(jnp.where(lower, 1.0, 0.0), decay, NT, HIGHEST)
    cum_row = dot(decay, jnp.where(row <= col, 1.0, 0.0), NN, HIGHEST)
    for h in range(heads):
        cols = slice(h * width, (h + 1) * width)
        query = query_ref[:, cols]
        scores = dot(query, key_ref[:, cols], NT)
        spread = cum_col[:, h : h + 1] - cum_row[h : h + 1, :]
        weights = jnp.where(lower, jnp.exp(jnp.where(lower, spread, 0.0)), 0.0)
        intra_ref[:, cols] = dot((scores * weights).astype(jnp.bfloat16), value_ref[:, cols], NN)
        scaled = query.astype(jnp.float32) * jnp.exp(cum_col[:, h : h + 1])
        scaled_ref[:, cols] = scaled.astype(jnp.bfloat16)
    factor_ref[...] = gain_ref[...] / (1.0 + jnp.exp(-gate_ref[...].astype(jnp.float32)))
    pick, first = picks(place_ref, ids_ref[...], block_rows, tokens)
    route = route_ref[...]
    weight = jnp.where(first, route[0:1, :], route[1:2, :])
    share_high_ref[...], share_low_ref[...] = two_parts(jnp.where(pick, weight, 0.0))


def post_kernel(
    back_ref,
    intra_ref,
    factor_ref,
    scaled_ref,
    share_high_ref,
    share_low_ref,
    attention_ref,
    moe_ref,
):
    block_rows = 2 * back_ref.shape[0]
    feat = moe_ref.shape[1]
    pieces = flat(back_ref[:, :, :feat])
    total = dot(share_high_ref[...], pieces, TN) + dot(share_low_ref[...], pieces, TN)
    moe_ref[...] = total.astype(jnp.bfloat16)
    width = 128
    heads = attention_ref.shape[1] // width
    per_head = block_rows // heads
    chunks = width // per_head
    for h in range(heads):
        cols = slice(h * width, (h + 1) * width)
        rows = slice(h * per_head // 2, (h + 1) * per_head // 2)
        state = jnp.concatenate(
            [
                flat(back_ref[rows, :, feat + i * width : feat + (i + 1) * width])
                for i in range(chunks)
            ],
            axis=0,
        )
        mixed = intra_ref[:, cols] + dot(scaled_ref[:, cols], state, NN)
        power = jnp.sum(mixed * mixed, axis=1, keepdims=True) * (1.0 / width)
        attention_ref[:, cols] = (mixed * lax.rsqrt(power + norm_eps) * factor_ref[:, cols]).astype(
            jnp.bfloat16
        )


def call(kernel, outs, scalars, cost, *arrays):
    specs = [pl.BlockSpec(memory_space=pltpu.SMEM)] * scalars
    specs += [pl.BlockSpec(memory_space=pltpu.VMEM)] * (len(arrays) - scalars)
    out_specs = [pl.BlockSpec(memory_space=pltpu.VMEM)] * len(outs)
    out_shape = [jax.ShapeDtypeStruct(shape, kind) for shape, kind in outs]
    if len(outs) == 1:
        out_specs, out_shape = out_specs[0], out_shape[0]
    return pl.pallas_call(
        kernel,
        in_specs=specs,
        out_specs=out_specs,
        out_shape=out_shape,
        cost_estimate=pl.CostEstimate(flops=cost, bytes_accessed=cost // 256, transcendentals=0),
        interpret=INTERPRET,
    )(*arrays)


def per_device(
    queries,
    key_input,
    value_input,
    out_gate,
    log_decay,
    norm_gain,
    features,
    expert_ids,
    route_weight,
    placement,
    gate_weight,
    up_weight,
    down_weight,
):
    seq_count = lax.axis_size("seq")
    head_count = lax.axis_size("head")
    tokens = queries.shape[0]
    heads_here = log_decay.shape[0]
    width = queries.shape[1] // heads_here
    feat = features.shape[1]
    ff = gate_weight.shape[1]
    bf16, f32 = jnp.bfloat16, jnp.float32
    lines = 2 * seq_count
    state_len = heads_here * width * width // lines
    ids = expert_ids.T
    swap = [(i, i ^ 1) for i in range(seq_count)]
    next_chip = [(i, i ^ 2) for i in range(seq_count)]

    outgoing = call(
        pre_kernel,
        [((seq_count, 2, feat + state_len + 64), bf16)],
        1,
        2**28,
        placement,
        key_input,
        value_input,
        log_decay,
        features,
        ids,
    )
    other_gate = lax.ppermute(gate_weight, "seq", swap)
    other_up = lax.ppermute(up_weight, "seq", swap)
    other_down = lax.ppermute(down_weight, "seq", swap)
    arrived = lax.all_to_all(
        outgoing, "seq", split_axis=0, concat_axis=0, tiled=True
    ).reshape(lines, -1)

    own_rows = arrived[:, :feat]
    near_rows = lax.ppermute(own_rows, "seq", next_chip)
    slot_rows = jnp.concatenate([own_rows, near_rows], axis=0)
    both_weight = jnp.concatenate([gate_weight, other_gate, up_weight, other_up], axis=1)
    gate_up = jnp.dot(slot_rows, both_weight, preferred_element_type=f32).astype(bf16)
    rows = slot_rows.shape[0]
    parts = lax.all_to_all(
        gate_up.reshape(head_count, rows // head_count, 4 * ff),
        "head",
        split_axis=0,
        concat_axis=0,
        tiled=True,
    )
    prefix_piece = call(scan_kernel, [((seq_count, 2, feat + state_len), bf16)], 0, 2**26, arrived)
    summed = jnp.sum(parts.astype(f32), axis=0)
    hidden_part = (jax.nn.silu(summed[:, : 2 * ff]) * summed[:, 2 * ff :]).astype(bf16)
    hidden = lax.all_to_all(
        jnp.broadcast_to(hidden_part[None], (head_count,) + hidden_part.shape),
        "head",
        split_axis=0,
        concat_axis=0,
        tiled=True,
    ).reshape(rows, 2 * ff)
    piece = jnp.dot(
        hidden,
        jnp.concatenate([down_weight, other_down], axis=0),
        preferred_element_type=f32,
    ).astype(bf16)
    near_piece = lax.ppermute(piece[lines:], "seq", next_chip)
    piece = (piece[:lines].astype(f32) + near_piece.astype(f32)).astype(bf16)
    leaving = lax.dynamic_update_slice(
        prefix_piece, piece.reshape(seq_count, 2, feat), (0, 0, 0)
    )
    returned = lax.all_to_all(
        leaving, "seq", split_axis=0, concat_axis=0, tiled=True
    )
    side = call(
        side_kernel,
        [
            ((tokens, heads_here * width), f32),
            ((tokens, heads_here * width), f32),
            ((tokens, heads_here * width), bf16),
            ((lines, tokens), bf16),
            ((lines, tokens), bf16),
        ],
        1,
        2**29,
        placement,
        queries,
        key_input,
        value_input,
        out_gate,
        log_decay,
        norm_gain.reshape(1, -1),
        ids,
        route_weight.T,
    )
    attention_out, moe_out = call(
        post_kernel,
        [((tokens, heads_here * width), bf16), ((tokens, feat), bf16)],
        0,
        2**28,
        returned,
        *side,
    )
    return (attention_out, moe_out)


def solution(mesh):
    placed = (
        P("seq", "head"),
        P("seq", "head"),
        P("seq", "head"),
        P("seq", "head"),
        P("head", "seq"),
        P("head"),
        P("seq", "head"),
        P("seq", None),
        P("seq", None),
        P(),
        P("head", "seq"),
        P("head", "seq"),
        P("seq", "head"),
    )

    return jax.shard_map(
        per_device,
        mesh=mesh,
        in_specs=placed,
        out_specs=(P("seq", "head"), P("seq", "head")),
        check_vma=False,
    )
```
